32 devices in a mesh: dp: 8 (over z, x), fsdp: 4 (over y, core).
Axes of the slice: x: 2, y: 2, z: 4, core: 2. Of those that a mesh axis runs over, the one named last changes fastest.
Arguments:
- tokens: bfloat16 [16, 2048, 768], P('dp', 'fsdp'), may hold values from -6 to 6
- teacher: bfloat16 [16, 2048, 768], P('dp', 'fsdp'), may hold values from -6 to 6
- lengths: int32 [16], replicated, may hold values from 256 to 2048, as said below
- dealing: int32 [16], replicated, may hold values from 0 to 15, as said below
- query_weight: bfloat16 [768, 768], P(('dp', 'fsdp')), may hold values from -0.4375 to 0.4375
- key_weight: bfloat16 [768, 768], P(('dp', 'fsdp')), may hold values from -0.21875 to 0.21875
- value_weight: bfloat16 [768, 768], P(('dp', 'fsdp')), may hold values from -0.21875 to 0.21875
- output_weight: bfloat16 [768, 768], P(('dp', 'fsdp')), may hold values from -0.875 to 0.875
- inner_weight: bfloat16 [768, 3072], P(('dp', 'fsdp')), may hold values from -0.21875 to 0.21875
- outer_weight: bfloat16 [3072, 768], P(('dp', 'fsdp')), may hold values from -0.109375 to 0.109375
- query_bias: bfloat16 [768], P(('dp', 'fsdp')), may hold values from -3 to 3
- value_bias: bfloat16 [768], P(('dp', 'fsdp')), may hold values from -3 to 3
- output_bias: bfloat16 [768], P(('dp', 'fsdp')), may hold values from -2 to 2
- norm_gain: bfloat16 [768], P(('dp', 'fsdp')), may hold values from 0.5 to 1.5
- norm_shift: bfloat16 [768], P(('dp', 'fsdp')), may hold values from -2 to 2
- inner_bias: bfloat16 [3072], P(('dp', 'fsdp')), may hold values from -3 to 3
- outer_bias: bfloat16 [768], P(('dp', 'fsdp')), may hold values from -2 to 2
- final_gain: bfloat16 [768], P(('dp', 'fsdp')), may hold values from 0.5 to 1.5
- final_shift: bfloat16 [768], P(('dp', 'fsdp')), may hold values from -2 to 2
Outputs:
- output: bfloat16 [16, 2048, 768], P('dp', 'fsdp')
- input_grad: bfloat16 [16, 2048, 768], P('dp', 'fsdp')
- grad_query_weight: float32 [768, 768], P(('dp', 'fsdp'))
- grad_key_weight: float32 [768, 768], P(('dp', 'fsdp'))
- grad_value_weight: float32 [768, 768], P(('dp', 'fsdp'))
- grad_output_weight: float32 [768, 768], P(('dp', 'fsdp'))
- grad_inner_weight: float32 [768, 3072], P(('dp', 'fsdp'))
- grad_outer_weight: float32 [3072, 768], P(('dp', 'fsdp'))
- grad_query_bias: float32 [768], P(('dp', 'fsdp'))
- grad_value_bias: float32 [768], P(('dp', 'fsdp'))
- grad_output_bias: float32 [768], P(('dp', 'fsdp'))
- grad_norm_gain: float32 [768], P(('dp', 'fsdp'))
- grad_norm_shift: float32 [768], P(('dp', 'fsdp'))
- grad_inner_bias: float32 [3072], P(('dp', 'fsdp'))
- grad_outer_bias: float32 [768], P(('dp', 'fsdp'))
- grad_final_gain: float32 [768], P(('dp', 'fsdp'))
- grad_final_shift: float32 [768], P(('dp', 'fsdp'))
The draws below stay inside these ranges and needn't reach their ends.
Inputs may be any that keep to these rules, and one draw needn't show every extreme that they name: `lengths`: the longest sequence has exactly 2048 valid tokens. `dealing`: a permutation of the 16 sequences; slots 2 g and 2 g + 1 hold one of the longer half and one of the shorter half of the sequences.
All inputs are finite; a program needn't handle non-finite values.
Results may differ from the reference program's by a relative error of at most 0.019.
Values may be sent and summed in bfloat16 or wider, within the bound.
No kernel may reach another device: no remote copies, remote signals or barrier semaphores. Data moves between devices by JAX's collectives and lax.ppermute only.
A program may use at most 256 MiB of HBM per device.

```python
import math
import jax
import jax.numpy as jnp
from jax import lax

D = 768
HEADS = 12
HD = 64
FF = 3072
SEQS = 16
LEN = 2048


def plan_sequences(key):
    base_key = jax.random.fold_in(key, 4099)
    key_lengths, key_longest, key_groups = jax.random.split(base_key, 3)
    drawn_lens = jax.random.randint(key_lengths, (SEQS,), LEN // 8, LEN + 1, dtype=jnp.int32)
    longest = jax.random.randint(key_longest, (), 0, SEQS, dtype=jnp.int32)
    places = jnp.arange(SEQS, dtype=jnp.int32)
    seq_lens = jnp.where(places == longest, LEN, drawn_lens).astype(jnp.int32)
    ranked = jnp.argsort(-(seq_lens * SEQS + places), stable=True).astype(jnp.int32)
    group_order = jax.random.permutation(key_groups, SEQS // 2).astype(jnp.int32)
    longer_half = ranked[:SEQS // 2]
    shorter_half = ranked[SEQS // 2:][::-1]
    dealt = jnp.zeros((SEQS,), jnp.int32)
    dealt = dealt.at[2 * group_order].set(longer_half)
    dealt = dealt.at[2 * group_order + 1].set(shorter_half)
    return (seq_lens, dealt)


def draw_lengths(key, part):
    return plan_sequences(key)[0]


def draw_dealing(key, part):
    return plan_sequences(key)[1]


def spiked(entries, key, source, target, shards_of, factor):
    owner, partner = [(jnp.arange(entries.shape[position]) // (entries.shape[position] // shards_of)).reshape([-1 if axis == position else 1 for axis in range(entries.ndim)]) for position in (source, target)]
    chosen = jax.random.permutation(key, shards_of)[partner]
    strong = (owner == chosen) | (owner == (partner + shards_of // 2) % shards_of)
    return jnp.where(strong, factor * entries, entries)


def shard_levels(key, dims, pieces, least, top_value):
    level = 1.0
    for position, blocks in pieces:
        heights = jax.random.uniform(jax.random.fold_in(jax.random.fold_in(key, 6), position), (blocks,), jnp.float32, least / len(pieces), top_value / len(pieces))
        level = level * jnp.repeat(jnp.exp(heights), dims[position] // blocks).reshape((-1,) + (1,) * (len(dims) - 1 - position))
    return level


def bell_draw(stream_key, extent, width, reach, cuts=(), held_as=jnp.bfloat16):
    array = jax.random.normal(stream_key, extent, jnp.float32) * width
    if len(cuts) > 0:
        array = shard_levels(stream_key, extent, cuts, -0.22, 0.18) * array
    return jnp.clip(array, min=-reach, max=reach).astype(held_as)


def gaussian_with(key, shape, deviation, bound, cuts, heavy, held_as=jnp.bfloat16):
    result = deviation * jax.random.normal(key, shape, jnp.float32)
    if cuts:
        result = result * shard_levels(key, shape, cuts, -0.22, 0.18)
    return jnp.clip(spiked(result, jax.random.fold_in(key, 3), *heavy), -bound, bound).astype(held_as)


def setup_inputs(seed: int = 0) -> dict:
    keys = jax.random.split(jax.random.key(seed), 20)
    tokens = bell_draw(keys[0], (SEQS, LEN, D), 1.0, 6.0, ((0, 8), (1, 4)))
    teacher = gaussian_with(keys[1], (SEQS, LEN, D), 1.0, 6.0, ((0, 8), (1, 4)), (0, 2, 8, 2.0))
    lengths = draw_lengths(jax.random.fold_in(keys[19], 71), 0)
    dealing = draw_dealing(jax.random.fold_in(keys[19], 71), 0)
    query_weight = bell_draw(keys[4], (D, D), (D // 4) ** -0.5, 0.4375, ((0, 32),))
    key_weight = bell_draw(keys[5], (D, D), D ** -0.5, 0.21875, ((0, 32),))
    value_weight = bell_draw(keys[6], (D, D), D ** -0.5, 0.21875, ((0, 32),))
    output_weight = bell_draw(keys[7], (D, D), (D // 16) ** -0.5, 0.875, ((0, 32),))
    inner_weight = bell_draw(keys[8], (D, FF), D ** -0.5, 0.21875, ((0, 32),))
    outer_weight = bell_draw(keys[9], (FF, D), FF ** -0.5, 0.109375, ((0, 32),))
    query_bias = bell_draw(keys[10], (D,), 0.5, 3.0, ((0, 32),))
    value_bias = bell_draw(keys[11], (D,), 0.5, 3.0, ((0, 32),))
    output_bias = bell_draw(keys[12], (D,), 0.3, 2.0, ((0, 32),))
    norm_gain = jnp.clip(1.0 + 0.1 * jax.random.normal(keys[13], (D,), jnp.float32), 0.5, 1.5).astype(jnp.bfloat16)
    norm_shift = bell_draw(keys[14], (D,), 0.3, 2.0, ((0, 32),))
    inner_bias = bell_draw(keys[15], (FF,), 0.5, 3.0, ((0, 32),))
    outer_bias = bell_draw(keys[16], (D,), 0.3, 2.0, ((0, 32),))
    final_gain = jnp.clip(1.0 + 0.1 * jax.random.normal(keys[17], (D,), jnp.float32), 0.5, 1.5).astype(jnp.bfloat16)
    final_shift = bell_draw(keys[18], (D,), 0.3, 2.0, ((0, 32),))
    return {"tokens": tokens, "teacher": teacher, "lengths": lengths, "dealing": dealing, "query_weight": query_weight, "key_weight": key_weight, "value_weight": value_weight, "output_weight": output_weight, "inner_weight": inner_weight, "outer_weight": outer_weight, "query_bias": query_bias, "value_bias": value_bias, "output_bias": output_bias, "norm_gain": norm_gain, "norm_shift": norm_shift, "inner_bias": inner_bias, "outer_bias": outer_bias, "final_gain": final_gain, "final_shift": final_shift}


epsilon = 1e-05
masked_score = -1e+30
highest = lax.Precision.HIGHEST

@jax.custom_vjp
def low(v):
    return lax.optimization_barrier(v.astype(jnp.bfloat16)).astype(jnp.float32)

@jax.custom_vjp
def low_back(v):
    return v

def low_keep(v):
    return (low(v), None)

def low_pass(kept, grad):
    return (grad,)

def back_keep(v):
    return (v, None)

def back_low(kept, grad):
    return (low(grad),)
low.defvjp(low_keep, low_pass)
low_back.defvjp(back_keep, back_low)

def round_both(value):
    return low_back(low(value))

def layer_norm(resid, gain, shift):
    average = lax.optimization_barrier(jnp.mean(resid, axis=-1, keepdims=True))
    centred = resid - average
    second = lax.optimization_barrier(jnp.mean(centred * centred, axis=-1, keepdims=True))
    return centred * lax.rsqrt(second + epsilon) * gain + shift

def product(left, right):
    return jnp.dot(left, right, precision=highest)

def attention_block(query_part, key_heads, value_heads, alive_mask, score_scale):
    scores = jnp.einsum('rhd,nhd->hrn', query_part, key_heads, precision=highest) * score_scale
    scores = low_back(scores)
    scores = jnp.where(alive_mask[None, None, :], scores, masked_score)
    probs = jax.nn.softmax(scores, axis=-1)
    return jnp.einsum('hrn,nhd->rhd', low(probs), value_heads, precision=highest)

def sequence_loss(seq_tokens, params, target, seq_length, loss_scale):
    w_query, w_key, w_value, w_output, w_inner, w_outer, b_query, b_value, b_output, gain_one, shift_one, b_inner, b_outer, gain_two, shift_two = params
    positions = lax.iota(jnp.int32, LEN)
    alive_mask = positions < seq_length
    score_scale = 1.0 / math.sqrt(HD)
    query_rows = round_both(product(seq_tokens, w_query) + b_query)
    key_rows = round_both(product(seq_tokens, w_key))
    value_rows = round_both(product(seq_tokens, w_value) + b_value)
    block_len = min(512, LEN)
    query_blocks = query_rows.reshape(LEN // block_len, block_len, HEADS, HD)
    key_heads = key_rows.reshape(LEN, HEADS, HD)
    value_heads = value_rows.reshape(LEN, HEADS, HD)
    block_fn = jax.checkpoint(lambda query_part: attention_block(query_part, key_heads, value_heads, alive_mask, score_scale))
    attn_rows = lax.map(block_fn, query_blocks).reshape(LEN, D)
    attn_rows = round_both(attn_rows)
    resid_one = seq_tokens + low_back(product(attn_rows, w_output) + b_output)
    hidden_rows = low(layer_norm(resid_one, gain_one, shift_one))
    inner_rows = low_back(product(hidden_rows, w_inner) + b_inner)
    act_rows = low(jax.nn.gelu(inner_rows, approximate=False))
    resid_two = hidden_rows + low_back(product(act_rows, w_outer) + b_outer)
    final_rows = layer_norm(resid_two, gain_two, shift_two)
    error_rows = (final_rows - target) * alive_mask[:, None].astype(jnp.float32)
    return (loss_scale * 0.5 * jnp.sum(error_rows * error_rows), final_rows)

def reference(tokens, teacher, lengths, dealing, query_weight, key_weight, value_weight, output_weight, inner_weight, outer_weight, query_bias, value_bias, output_bias, norm_gain, norm_shift, inner_bias, outer_bias, final_gain, final_shift):
    params = tuple((weight.astype(jnp.float32) for weight in (query_weight, key_weight, value_weight, output_weight, inner_weight, outer_weight, query_bias, value_bias, output_bias, norm_gain, norm_shift, inner_bias, outer_bias, final_gain, final_shift)))
    count_valid = jnp.sum(lengths).astype(jnp.float32)
    loss_scale = SEQS * LEN / count_valid
    work_tokens = jnp.take(tokens, dealing, axis=0)
    work_lens = jnp.take(lengths, dealing)
    zero_grads = jax.tree.map(jnp.zeros_like, params)

    def advance(running, item):
        seq_tokens, target, seq_length = item
        token_float = seq_tokens.astype(jnp.float32)
        target_float = target.astype(jnp.float32)

        def loss_fn(inputs, weights):
            return sequence_loss(inputs, weights, target_float, seq_length, loss_scale)
        loss_value, pull_back, final_rows = jax.vjp(loss_fn, token_float, params, has_aux=True)
        grad_tokens, grad_params = pull_back(jnp.ones((), jnp.float32))
        running = jax.tree.map(jnp.add, running, grad_params)
        return (running, (final_rows.astype(jnp.bfloat16), grad_tokens.astype(jnp.bfloat16)))
    grads, (work_out, work_grad) = lax.scan(advance, zero_grads, (work_tokens, teacher, work_lens))
    output = jnp.zeros_like(tokens).at[dealing].set(work_out)
    input_grad = jnp.zeros_like(tokens).at[dealing].set(work_grad)
    return (output, input_grad, grads[0], grads[1], grads[2], grads[3], grads[4], grads[5], grads[6], grads[7], grads[8], grads[9], grads[10], grads[11], grads[12], grads[13], grads[14])
```

```python
import functools
import math

import jax
import jax.numpy as jnp
from jax import lax
from jax.experimental import pallas as pl
from jax.experimental.pallas import tpu as pltpu
from jax.sharding import PartitionSpec as P

HEADS = 12
EPSILON = 1e-05
MASKED = -1e30
LOG2E = 1.4426950408889634
BOTH = ("dp", "fsdp")
NN = (((1,), (0,)), ((), ()))
NT = (((1,), (1,)), ((), ()))
TN = (((0,), (0,)), ((), ()))
f32 = jnp.float32
bf16 = jnp.bfloat16
LANES = 128


def dot(left, right, dims=NN, precision=None):
    return lax.dot_general(left, right, dims, preferred_element_type=f32, precision=precision)


def attend_kernel(q_ref, k_ref, v_ref, bias_ref, o_ref, lse_ref, k_even, k_odd, v_even, v_odd, *, scale):
    half = LANES // 2

    @pl.when(pl.program_id(1) == 0)
    def _():
        k, v, bias = k_ref[...], v_ref[...], bias_ref[...]
        low = lax.broadcasted_iota(jnp.int32, k.shape, 1) < half
        one = jnp.ones_like(v)
        k_even[...] = jnp.where(low, k, bias)
        k_odd[...] = jnp.where(low, bias, k)
        v_even[...] = jnp.where(low, v, one)
        v_odd[...] = jnp.where(low, one, v)

    q = q_ref[...]
    lane = lax.broadcasted_iota(jnp.int32, q.shape, 1)
    low = lane < half
    scaled = q * jnp.asarray(scale, bf16)
    one, zero = jnp.ones_like(q), jnp.zeros_like(q)
    q_even = jnp.where(low, scaled, jnp.where(lane == half, one, zero))
    q_odd = jnp.where(low, jnp.where(lane == 0, one, zero), scaled)

    def head(queries, keys, values):
        scores = dot(queries, keys[...], NT)
        top = jnp.max(scores, axis=1, keepdims=True)
        weights = jnp.exp2((scores - top) * LOG2E)
        return dot(weights.astype(bf16), values[...]), top

    out_even, top_even = head(q_even, k_even, v_even)
    out_odd, top_odd = head(q_odd, k_odd, v_odd)
    out = jnp.where(low, out_even, out_odd)
    total = jnp.where(low, pltpu.roll(out_even, half, 1), pltpu.roll(out_odd, half, 1))
    o_ref[...] = (out / total).astype(o_ref.dtype)
    lse = (jnp.where(low, top_even, top_odd) + jnp.log(total)) * LOG2E
    row = lax.broadcasted_iota(jnp.int32, (8, LANES), 0)
    col = lax.broadcasted_iota(jnp.int32, (8, LANES), 1)
    pick = jnp.where(col == row * half, 1.0, 0.0).astype(f32)
    lse_ref[0] = dot(pick, lse, NT, lax.Precision.HIGHEST)


def attend(qkv, bias, width, scale, block):
    rows = qkv.shape[0]
    pairs = width // LANES
    spec = lambda part: pl.BlockSpec((rows, LANES), lambda h, i: (0, part * pairs + h))
    return pl.pallas_call(
        functools.partial(attend_kernel, scale=scale),
        grid=(pairs, rows // block),
        in_specs=[
            pl.BlockSpec((block, LANES), lambda h, i: (i, h)),
            spec(1),
            spec(2),
            pl.BlockSpec((rows, LANES), lambda h, i: (0, 0)),
        ],
        out_specs=[
            pl.BlockSpec((block, LANES), lambda h, i: (i, h)),
            pl.BlockSpec((1, 8, block), lambda h, i: (h, 0, i)),
        ],
        out_shape=[
            jax.ShapeDtypeStruct((rows, width), bf16),
            jax.ShapeDtypeStruct((pairs, 8, rows), f32),
        ],
        scratch_shapes=[pltpu.VMEM((rows, LANES), bf16)] * 4,
        compiler_params=pltpu.CompilerParams(vmem_limit_bytes=56 << 20),
        cost_estimate=pl.CostEstimate(
            flops=4 * rows * rows * width * 4,
            bytes_accessed=8 * rows * width,
            transcendentals=rows * rows * pairs * 2,
        ),
        name="attend",
    )(qkv, qkv, qkv, bias)


def attend_back_kernel(
    q_ref, k_ref, v_ref, bias_ref, do_ref, o_ref, lse_ref,
    dq_ref, dk_ref, dv_ref,
    q_even, q_odd, z_even, z_odd, d_even, d_odd, delta, dq_turned,
    *, scale, block,
):
    half = LANES // 2
    step = pl.program_id(1)
    rows = q_ref.shape[0]

    @pl.when(step == 0)
    def _():
        lane = lax.broadcasted_iota(jnp.int32, q_ref.shape, 1)
        low = lane < half
        scaled = q_ref[...] * jnp.asarray(scale, bf16)
        one, zero = jnp.ones_like(scaled), jnp.zeros_like(scaled)
        q_even[...] = jnp.where(low, scaled, jnp.where(lane == half, one, zero))
        q_odd[...] = jnp.where(low, jnp.where(lane == 0, one, zero), scaled)
        z_even[...] = jnp.where(low, scaled, zero)
        z_odd[...] = jnp.where(low, zero, scaled)
        grad = do_ref[...]
        d_even[...] = jnp.where(low, grad, zero)
        d_odd[...] = jnp.where(low, zero, grad)
        row = lax.broadcasted_iota(jnp.int32, (8, LANES), 0)
        col = lax.broadcasted_iota(jnp.int32, (8, LANES), 1)
        select = jnp.where(lax.div(col, half) == row, 1.0, 0.0).astype(f32)
        product = grad.astype(f32) * o_ref[...].astype(f32)
        delta[...] = dot(select, product, NT, lax.Precision.HIGHEST)
        dq_turned[...] = jnp.zeros_like(dq_turned)

    k, v, bias = k_ref[...], v_ref[...], bias_ref[...]
    low = lax.broadcasted_iota(jnp.int32, k.shape, 1) < half
    k_even = jnp.where(low, k, bias)
    k_odd = jnp.where(low, bias, k)
    k_turned = k.T
    dk = jnp.zeros(k.shape, f32)
    dv = jnp.zeros(k.shape, f32)
    heads = ((k_even, q_even, z_even, d_even), (k_odd, q_odd, z_odd, d_odd))
    for first in range(0, rows, block):
        part = slice(first, first + block)
        for h, (keys, queries, plain, grads) in enumerate(heads):
            scores = dot(keys, queries[part, :], NT)
            weights = jnp.exp2(scores * LOG2E - lse_ref[0, h : h + 1, part])
            d_weights = dot(v, grads[part, :], NT)
            d_scores = (weights * (d_weights - delta[h : h + 1, part])).astype(bf16)
            dv += dot(weights.astype(bf16), grads[part, :])
            dk += dot(d_scores, plain[part, :])
            dq_turned[h * half : (h + 1) * half, part] += dot(
                k_turned[h * half : (h + 1) * half, :], d_scores
            )
    dk_ref[...] = dk.astype(bf16)
    dv_ref[...] = dv.astype(bf16)

    @pl.when(step == pl.num_programs(1) - 1)
    def _():
        dq_ref[...] = (dq_turned[...] * scale).T.astype(bf16)


def attend_back(qkv, bias, grads, out, lse, width, scale, key_block, block):
    rows = qkv.shape[0]
    pairs = width // LANES
    whole = lambda: pl.BlockSpec((rows, LANES), lambda h, j: (0, h))
    part = lambda n: pl.BlockSpec((key_block, LANES), lambda h, j: (j, n * pairs + h))
    return pl.pallas_call(
        functools.partial(attend_back_kernel, scale=scale, block=block),
        grid=(pairs, rows // key_block),
        in_specs=[
            whole(),
            part(1),
            part(2),
            pl.BlockSpec((key_block, LANES), lambda h, j: (j, 0)),
            whole(),
            whole(),
            pl.BlockSpec((1, 8, rows), lambda h, j: (h, 0, 0)),
        ],
        out_specs=[whole(), part(0), part(0)],
        out_shape=[jax.ShapeDtypeStruct((rows, width), bf16)] * 3,
        scratch_shapes=[pltpu.VMEM((rows, LANES), bf16)] * 6
        + [pltpu.VMEM((8, rows), f32), pltpu.VMEM((LANES, rows), f32)],
        compiler_params=pltpu.CompilerParams(vmem_limit_bytes=56 << 20),
        cost_estimate=pl.CostEstimate(
            flops=10 * rows * rows * width * 4,
            bytes_accessed=16 * rows * width,
            transcendentals=rows * rows * pairs * 2,
        ),
        name="attend_back",
    )(qkv, qkv, qkv, bias, grads, out, lse)


DIGITS = {"z": (4, 8), "x": (2, 4), "y": (2, 2), "c": (2, 1)}


def digit(name):
    size, stride = DIGITS[name]
    number = lax.axis_index("dp") * 4 + lax.axis_index("fsdp")
    return lax.rem(lax.div(number, stride), size)


def shift(value, name, amount):
    size, stride = DIGITS[name]
    pairs = []
    for source in range(32):
        place = source // stride % size
        pairs.append((source, source + ((place + amount) % size - place) * stride))
    return lax.ppermute(value, BOTH, pairs)


def gather_z(part):
    ring = [part] + [shift(part, "z", amount) for amount in (3, 2, 1)]
    ring = jnp.stack(ring + ring[:-1])
    return lax.dynamic_slice_in_dim(ring, lax.rem(4 - digit("z"), 4), 4, 0)


def spread(part, order):
    held = {(): gather_z(part)}
    for name in order:
        arrived = {key + (1,): shift(value, name, 1) for key, value in held.items()}
        held = {key + (0,): value for key, value in held.items()}
        held.update(arrived)
    return held


def put_together(held, order):
    first = next(iter(held.values()))
    out = jnp.zeros((4, 2, 2, 2) + first.shape[1:], first.dtype)
    own = {name: digit(name) for name in "xyc"}
    for key, value in held.items():
        place = {name: own[name] ^ rel for name, rel in zip(order, key)}
        start = (0, place["x"], place["y"], place["c"]) + (0,) * (first.ndim - 1)
        out = lax.dynamic_update_slice(out, value[:, None, None, None], start)
    return out.reshape((32 * first.shape[1],) + first.shape[2:])


def gather_rows(part, order):
    if lax.axis_size("dp") == 8 and lax.axis_size("fsdp") == 4:
        return put_together(spread(part, order + "c"), order + "c")
    return lax.all_gather(part, BOTH, axis=0, tiled=True)


def pick(value, axis, index):
    return lax.squeeze(lax.dynamic_slice_in_dim(value, index, 1, axis), (axis,))


def halve(value, axes, name):
    axis = axes.index(name)
    own = digit(name)
    arrived = shift(pick(value, axis, 1 - own).astype(bf16), name, 1)
    kept = pick(value, axis, own).astype(f32) + arrived.astype(f32)
    return kept, axes[:axis] + axes[axis + 1 :]


def scatter_rows(value, order):
    if not (lax.axis_size("dp") == 8 and lax.axis_size("fsdp") == 4):
        return lax.psum_scatter(value, BOTH, scatter_dimension=0, tiled=True)
    rows = value.shape[0] // 32
    value = value.reshape((4, 2, 2, 2, rows, value.shape[1]))
    axes = "zxyc"
    for name in "c" + order:
        value, axes = halve(value, axes, name)
    return scatter_z(value)


def scatter_z(value):
    own = digit("z")
    total = pick(value, 0, own).astype(f32)
    for amount in (1, 2, 3):
        piece = pick(value, 0, lax.rem(own + amount, 4)).astype(bf16)
        total = total + shift(piece, "z", amount).astype(f32)
    return total


def normalize(resid):
    average = jnp.mean(resid, axis=-1, keepdims=True)
    centred = resid - average
    second = jnp.mean(centred * centred, axis=-1, keepdims=True)
    inverse = lax.rsqrt(second + EPSILON)
    return centred * inverse, inverse


def normalize_back(grad, unit, inverse, gain):
    scaled = grad * gain
    along = jnp.mean(scaled * unit, axis=-1, keepdims=True)
    return inverse * (scaled - jnp.mean(scaled, axis=-1, keepdims=True) - unit * along)


def shards(
    tokens, teacher, lengths, dealing,
    query_weight, key_weight, value_weight, output_weight, inner_weight, outer_weight,
    query_bias, value_bias, output_bias, norm_gain, norm_shift, inner_bias, outer_bias,
    final_gain, final_shift,
):
    slots, row_count, width = tokens.shape
    sections = lax.axis_size("fsdp")
    dp_count = lax.axis_size("dp")
    ranks = sections // 2
    fast = dp_count == 8 and sections == 4
    hidden_units = inner_weight.shape[1]
    head_width = width // HEADS
    scale = 1.0 / math.sqrt(head_width)
    seq_total = lengths.shape[0]
    seq_len = row_count * sections
    share = width // ranks
    padded = -(-share // LANES) * LANES
    rows = 2 * row_count

    place = lax.axis_index("fsdp")
    side = lax.div(place, ranks)
    rank = lax.rem(place, ranks)
    across = [(f, (f + ranks) % sections) for f in range(sections)]
    groups = [[g * ranks + r for r in range(ranks)] for g in range(2)]
    partner = [(f, f ^ 1) for f in range(sections)]
    length = lax.dynamic_index_in_dim(
        lengths, lax.axis_index("dp") * slots + side, keepdims=False
    )

    def swap_in(whole):
        kept = lax.dynamic_index_in_dim(whole, side, 0, keepdims=False)
        sent = lax.dynamic_index_in_dim(whole, 1 - side, 0, keepdims=False)
        return jnp.concatenate([kept, lax.ppermute(sent, "fsdp", across)], axis=0)

    def swap_out(local):
        kept = local[:row_count]
        arrived = lax.ppermute(local[row_count:], "fsdp", across)
        return jnp.where(side == 0, jnp.stack([kept, arrived]), jnp.stack([arrived, kept]))

    def gather_group(local):
        if ranks == 2:
            return jnp.concatenate([local, lax.ppermute(local, "fsdp", partner)], axis=0)
        return lax.all_gather(local, "fsdp", axis=0, tiled=True, axis_index_groups=groups)

    if ranks == 2:
        rank_order = [rank, 1 - rank]
    else:
        rank_order = [jnp.int32(r) for r in range(ranks)]
    block_ids = []
    for r in rank_order:
        block_ids += [side * ranks + r, (1 - side) * ranks + r]
    within = lax.iota(jnp.int32, row_count)
    positions = jnp.concatenate([b * row_count + within for b in block_ids])
    bias = jnp.where(positions < length, 0.0, MASKED).astype(bf16)
    key_bias = jnp.broadcast_to(bias[:, None], (rows * ranks, LANES))

    def heads_to_rows(part):
        if ranks == 2:
            kept = part[:rows]
            arrived = lax.ppermute(part[rows:], "fsdp", partner)
            return jnp.where(
                rank == 0,
                jnp.concatenate([kept, arrived], axis=1),
                jnp.concatenate([arrived, kept], axis=1),
            )
        return lax.all_to_all(
            part, "fsdp", split_axis=0, concat_axis=1, tiled=True, axis_index_groups=groups
        )

    def rows_to_heads(part):
        if ranks == 2:
            kept = lax.dynamic_slice_in_dim(part, rank * share, share, 1)
            sent = lax.dynamic_slice_in_dim(part, (1 - rank) * share, share, 1)
            return jnp.concatenate([kept, lax.ppermute(sent, "fsdp", partner)], axis=0)
        return lax.all_to_all(
            part, "fsdp", split_axis=1, concat_axis=0, tiled=True, axis_index_groups=groups
        )

    vectors = [
        query_bias, value_bias, output_bias, norm_gain, norm_shift, outer_bias, final_gain,
        final_shift, inner_bias,
    ]
    packed = jnp.concatenate(vectors)
    small = query_weight.shape[0]
    if fast:
        per_row = packed.shape[0] // small
        packed = jnp.pad(packed.reshape(small, per_row), ((0, 0), (0, LANES - per_row)))
        first = jnp.concatenate([query_weight, key_weight, value_weight, packed], axis=1)
        held = spread(first, "xy")

        def mine(block, which):
            parts = [
                lax.dynamic_slice_in_dim(block, n * width + which * share, share, 2)
                for n in range(3)
            ]
            return jnp.concatenate(parts + [block[:, :, 3 * width :]], axis=2)

        last = {}
        for key, block in held.items():
            last[key + (0,)] = mine(block, rank)
            last[key + (1,)] = shift(mine(block, 1 - rank), "c", 1)
        whole = put_together(last, "xyc")
        qkv_weight = whole[:, : 3 * share]
        packed = whole[:, 3 * share : 3 * share + per_row].reshape(32, small * per_row)
    else:
        whole = [
            lax.all_gather(w, BOTH, axis=0, tiled=True)
            for w in (query_weight, key_weight, value_weight)
        ]
        whole = [lax.dynamic_slice_in_dim(w, rank * share, share, 1) for w in whole]
        qkv_weight = jnp.concatenate(whole, axis=1)
        packed = lax.all_gather(packed, BOTH, axis=0, tiled=False).reshape(
            dp_count * sections, packed.shape[0]
        )
    unpacked = []
    start = 0
    for vector in vectors:
        count = vector.shape[0]
        unpacked.append(packed[:, start : start + count].reshape(-1).astype(f32))
        start += count
    b_query, b_value, b_output, gain_one, shift_one, b_outer, gain_two, shift_two, b_inner = unpacked
    w_output = gather_rows(output_weight, "xy")
    w_inner = gather_rows(inner_weight, "xy")
    w_outer = gather_rows(outer_weight, "yx")

    local = swap_in(tokens)
    gathered = gather_group(local)
    b_qkv = jnp.concatenate(
        [
            lax.dynamic_slice_in_dim(b_query, rank * share, share),
            jnp.zeros((share,), f32),
            lax.dynamic_slice_in_dim(b_value, rank * share, share),
        ]
    )
    qkv = (dot(gathered, qkv_weight) + b_qkv).astype(bf16)
    if padded != share:
        fill = ((0, 0), (0, 0), (0, padded - share))
        qkv = jnp.pad(qkv.reshape(-1, 3, share), fill).reshape(-1, 3 * padded)
    heads_out, lse = attend(qkv, key_bias, padded, scale, 1024)
    attn_rows = heads_to_rows(heads_out[:, :share])

    resid_one = local.astype(f32) + dot(attn_rows, w_output) + b_output
    unit_one, inverse_one = normalize(resid_one)
    hidden = (unit_one * gain_one + shift_one).astype(bf16)
    inner = dot(hidden, w_inner) + b_inner
    normal = 0.5 + 0.5 * lax.erf(inner * math.sqrt(0.5))
    act = (inner * normal).astype(bf16)
    slope = (normal + inner * jnp.exp(-0.5 * inner * inner) * (1.0 / math.sqrt(2 * math.pi))).astype(bf16)
    resid_two = hidden.astype(f32) + dot(act, w_outer) + b_outer
    unit_two, inverse_two = normalize(resid_two)
    final = unit_two * gain_two + shift_two
    output = swap_out(final.astype(bf16))

    slot_ids = lax.iota(jnp.int32, seq_total)
    inverse = jnp.sum(
        jnp.where(dealing[None, :] == slot_ids[:, None], slot_ids[None, :], 0), axis=1
    )
    target = lax.all_to_all(teacher, "dp", split_axis=1, concat_axis=0, tiled=True)
    target = jnp.take(target, inverse, axis=0)
    target = lax.all_to_all(target, "dp", split_axis=0, concat_axis=1, tiled=True)
    target = swap_in(target)

    valid = (positions[:rows] < length).astype(f32)[:, None] if ranks == 2 else None
    if valid is None:
        own = jnp.concatenate(
            [b * row_count + within for b in (side * ranks + rank, (1 - side) * ranks + rank)]
        )
        valid = (own < length).astype(f32)[:, None]
    loss_scale = seq_total * seq_len / jnp.sum(lengths).astype(f32)
    grad_final = loss_scale * (final - target.astype(f32)) * valid
    grad_gain_two = jnp.sum(grad_final * unit_two, axis=0)
    grad_shift_two = jnp.sum(grad_final, axis=0)
    d_two = normalize_back(grad_final, unit_two, inverse_two, gain_two)
    d_out = d_two.astype(bf16)
    grad_outer_bias = jnp.sum(d_out.astype(f32), axis=0)
    d_inner = (dot(d_out, w_outer, NT) * slope.astype(f32)).astype(bf16)
    grad_inner_bias = jnp.sum(d_inner.astype(f32), axis=0)
    d_hidden = d_two + dot(d_inner, w_inner, NT)
    grad_gain_one = jnp.sum(d_hidden * unit_one, axis=0)
    grad_shift_one = jnp.sum(d_hidden, axis=0)
    d_one = normalize_back(d_hidden, unit_one, inverse_one, gain_one)
    d_mix = d_one.astype(bf16)
    grad_output_bias = jnp.sum(d_mix.astype(f32), axis=0)
    d_attn = dot(d_mix, w_output, NT).astype(bf16)
    heads_grad = rows_to_heads(d_attn)

    grad_outer = scatter_rows(dot(act, d_out, TN), "yx")
    grad_inner = scatter_rows(dot(hidden, d_inner, TN), "xy")
    grad_output = scatter_rows(dot(attn_rows, d_mix, TN), "yx")

    if padded != share:
        heads_grad = jnp.pad(heads_grad, ((0, 0), (0, padded - share)))
    d_query, d_key, d_value = attend_back(
        qkv, key_bias, heads_grad, heads_out, lse, padded, scale, 512, 1024
    )
    d_query, d_key, d_value = d_query[:, :share], d_key[:, :share], d_value[:, :share]
    d_qkv = jnp.concatenate([d_query, d_key, d_value], axis=1)
    grad_qkv = dot(gathered, d_qkv, TN)
    bias_query = jnp.sum(d_query.astype(f32), axis=0)
    bias_value = jnp.sum(d_value.astype(f32), axis=0)
    d_gathered = dot(d_qkv, qkv_weight, NT)
    if ranks == 2:
        arrived = lax.ppermute(d_gathered[rows:].astype(bf16), "fsdp", partner)
        d_local = d_gathered[:rows] + arrived.astype(f32)
    else:
        d_local = lax.psum_scatter(
            d_gathered, "fsdp", scatter_dimension=0, tiled=True, axis_index_groups=groups
        )
    input_grad = swap_out((d_one + d_local).astype(bf16))

    def place_share(part):
        empty = jnp.zeros(part.shape[:-1] + (width,), part.dtype)
        return lax.dynamic_update_slice_in_dim(empty, part, rank * share, part.ndim - 1)

    sums = [
        place_share(bias_query), place_share(bias_value), grad_output_bias, grad_gain_one,
        grad_shift_one, grad_outer_bias, grad_gain_two, grad_shift_two, grad_inner_bias,
    ]
    sums = jnp.concatenate([s.reshape(dp_count * sections, -1) for s in sums], axis=1)
    if fast:
        value = grad_qkv.reshape(4, 2, 2, 2 * small, 3 * share)
        axes = "zxy"
        for name in "xy":
            value, axes = halve(value, axes, name)
        value = scatter_z(value).reshape(2, small, 3, share)
        own = pick(value, 0, rank)
        arrived = shift(pick(value, 0, 1 - rank), "c", 1)
        value = jnp.where(
            rank == 0,
            jnp.concatenate([own, arrived], axis=2),
            jnp.concatenate([arrived, own], axis=2),
        )
        grad_query, grad_key, grad_value = value[:, 0], value[:, 1], value[:, 2]
        small_sums = sums.reshape(4, 2, 2, 2, 1, sums.shape[1])
        axes = "zxyc"
        for name in "cxy":
            axis = axes.index(name)
            own = digit(name)
            small_sums = pick(small_sums, axis, own) + shift(
                pick(small_sums, axis, 1 - own), name, 1
            )
            axes = axes[:axis] + axes[axis + 1 :]
        own = digit("z")
        total = pick(small_sums, 0, own)
        for amount in (1, 2, 3):
            total = total + shift(
                pick(small_sums, 0, lax.rem(own + amount, 4)), "z", amount
            )
        sums = total.reshape(-1)
    else:
        parts = [place_share(grad_qkv[:, n * share : (n + 1) * share]) for n in range(3)]
        grad_query, grad_key, grad_value = [
            lax.psum_scatter(p, BOTH, scatter_dimension=0, tiled=True) for p in parts
        ]
        sums = lax.psum_scatter(sums, BOTH, scatter_dimension=0, tiled=True).reshape(-1)
    split = []
    start = 0
    for vector in vectors:
        count = vector.shape[0]
        split.append(sums[start : start + count])
        start += count
    return (
        output, input_grad, grad_query, grad_key, grad_value, grad_output, grad_inner, grad_outer,
        split[0], split[1], split[2], split[3], split[4], split[8], split[5], split[6], split[7],
    )


def solution(mesh):
    act = P("dp", "fsdp", None)
    matrix = P(BOTH, None)
    vector = P(BOTH)
    return jax.shard_map(
        shards,
        mesh=mesh,
        in_specs=(act, act, P(), P()) + (matrix,) * 6 + (vector,) * 9,
        out_specs=(act, act) + (matrix,) * 6 + (vector,) * 9,
        check_vma=False,
    )
```

```python
import functools
import math

import jax
import jax.numpy as jnp
from jax import lax
from jax.experimental import pallas as pl
from jax.experimental.pallas import tpu as pltpu
from jax.sharding import PartitionSpec as P

HEADS = 12
EPSILON = 1e-05
MASKED = -1e30
LOG2E = 1.4426950408889634
BOTH = ("dp", "fsdp")
NN = (((1,), (0,)), ((), ()))
NT = (((1,), (1,)), ((), ()))
TN = (((0,), (0,)), ((), ()))
f32 = jnp.float32
bf16 = jnp.bfloat16
LANES = 128


def dot(left, right, dims=NN, precision=None):
    return lax.dot_general(left, right, dims, preferred_element_type=f32, precision=precision)


def attend_kernel(q_ref, k_ref, v_ref, bias_ref, o_ref, lse_ref, k_even, k_odd, v_even, v_odd, *, scale):
    half = LANES // 2

    @pl.when(pl.program_id(1) == 0)
    def _():
        k, v, bias = k_ref[...], v_ref[...], bias_ref[...]
        low = lax.broadcasted_iota(jnp.int32, k.shape, 1) < half
        one = jnp.ones_like(v)
        k_even[...] = jnp.where(low, k, bias)
        k_odd[...] = jnp.where(low, bias, k)
        v_even[...] = jnp.where(low, v, one)
        v_odd[...] = jnp.where(low, one, v)

    q = q_ref[...]
    lane = lax.broadcasted_iota(jnp.int32, q.shape, 1)
    low = lane < half
    scaled = q * jnp.asarray(scale, bf16)
    one, zero = jnp.ones_like(q), jnp.zeros_like(q)
    q_even = jnp.where(low, scaled, jnp.where(lane == half, one, zero))
    q_odd = jnp.where(low, jnp.where(lane == 0, one, zero), scaled)

    def head(queries, keys, values):
        scores = dot(queries, keys[...], NT)
        top = jnp.max(scores, axis=1, keepdims=True)
        weights = jnp.exp2((scores - top) * LOG2E)
        return dot(weights.astype(bf16), values[...]), top

    out_even, top_even = head(q_even, k_even, v_even)
    out_odd, top_odd = head(q_odd, k_odd, v_odd)
    out = jnp.where(low, out_even, out_odd)
    total = jnp.where(low, pltpu.roll(out_even, half, 1), pltpu.roll(out_odd, half, 1))
    o_ref[...] = (out / total).astype(o_ref.dtype)
    lse = (jnp.where(low, top_even, top_odd) + jnp.log(total)) * LOG2E
    row = lax.broadcasted_iota(jnp.int32, (8, LANES), 0)
    col = lax.broadcasted_iota(jnp.int32, (8, LANES), 1)
    pick = jnp.where(col == row * half, 1.0, 0.0).astype(f32)
    lse_ref[0] = dot(pick, lse, NT, lax.Precision.HIGHEST)


def attend(qkv, bias, first, count, scale, block):
    rows = qkv.shape[0]
    whole = lambda n: pl.BlockSpec((rows, LANES), lambda h, i: (0, 3 * (first + h) + n))
    return pl.pallas_call(
        functools.partial(attend_kernel, scale=scale),
        grid=(count, rows // block),
        in_specs=[
            pl.BlockSpec((block, LANES), lambda h, i: (i, 3 * (first + h))),
            whole(1),
            whole(2),
            pl.BlockSpec((rows, LANES), lambda h, i: (0, 0)),
        ],
        out_specs=[
            pl.BlockSpec((block, LANES), lambda h, i: (i, h)),
            pl.BlockSpec((1, 8, block), lambda h, i: (h, 0, i)),
        ],
        out_shape=[
            jax.ShapeDtypeStruct((rows, count * LANES), bf16),
            jax.ShapeDtypeStruct((count, 8, rows), f32),
        ],
        scratch_shapes=[pltpu.VMEM((rows, LANES), bf16)] * 4,
        compiler_params=pltpu.CompilerParams(vmem_limit_bytes=56 << 20),
        cost_estimate=pl.CostEstimate(
            flops=16 * rows * rows * LANES * count,
            bytes_accessed=8 * rows * LANES * count,
            transcendentals=rows * rows * 2 * count,
        ),
        name="attend",
    )(qkv, qkv, qkv, bias)


def attend_back_kernel(
    q_ref, k_ref, v_ref, bias_ref, do_ref, o_ref, lse_ref, x_ref, *rest, scale, block,
):
    grad_ref, weight_ref, q_even, q_odd, z_even, z_odd, d_even, d_odd, delta, dq_turned, x_here, arrival = rest[-12:]
    fetch = pltpu.make_async_copy(x_ref, x_here, arrival)
    half = LANES // 2
    step = pl.program_id(0)
    rows = q_ref.shape[0]

    @pl.when(step == 0)
    def _():
        fetch.start()
        lane = lax.broadcasted_iota(jnp.int32, q_ref.shape, 1)
        low = lane < half
        scaled = q_ref[...] * jnp.asarray(scale, bf16)
        one, zero = jnp.ones_like(scaled), jnp.zeros_like(scaled)
        q_even[...] = jnp.where(low, scaled, jnp.where(lane == half, one, zero))
        q_odd[...] = jnp.where(low, jnp.where(lane == 0, one, zero), scaled)
        z_even[...] = jnp.where(low, scaled, zero)
        z_odd[...] = jnp.where(low, zero, scaled)
        grad = do_ref[...]
        d_even[...] = jnp.where(low, grad, zero)
        d_odd[...] = jnp.where(low, zero, grad)
        row = lax.broadcasted_iota(jnp.int32, (8, LANES), 0)
        col = lax.broadcasted_iota(jnp.int32, (8, LANES), 1)
        select = jnp.where(lax.div(col, half) == row, 1.0, 0.0).astype(f32)
        product = grad.astype(f32) * o_ref[...].astype(f32)
        delta[...] = dot(select, product, NT, lax.Precision.HIGHEST)
        dq_turned[...] = jnp.zeros_like(dq_turned)

    k, v, bias = k_ref[...], v_ref[...], bias_ref[...]
    low = lax.broadcasted_iota(jnp.int32, k.shape, 1) < half
    k_even = jnp.where(low, k, bias)
    k_odd = jnp.where(low, bias, k)
    k_turned = k.T
    dk = jnp.zeros(k.shape, f32)
    dv = jnp.zeros(k.shape, f32)
    heads = ((k_even, q_even, z_even, d_even), (k_odd, q_odd, z_odd, d_odd))
    for first in range(0, rows, block):
        part = slice(first, first + block)
        for h, (keys, queries, plain, grads) in enumerate(heads):
            scores = dot(keys, queries[part, :], NT)
            weights = jnp.exp2(scores * LOG2E - lse_ref[0, h : h + 1, part])
            d_weights = dot(v, grads[part, :], NT)
            d_scores = (weights * (d_weights - delta[h : h + 1, part])).astype(bf16)
            dv += dot(weights.astype(bf16), grads[part, :])
            dk += dot(d_scores, plain[part, :])
            dq_turned[h * half : (h + 1) * half, part] += dot(
                k_turned[h * half : (h + 1) * half, :], d_scores
            )
    here = pl.ds(pl.multiple_of(step * k.shape[0], k.shape[0]), k.shape[0])
    grad_ref[here, LANES : 2 * LANES] = dk.astype(bf16)
    grad_ref[here, 2 * LANES :] = dv.astype(bf16)

    @pl.when(step == pl.num_programs(0) - 1)
    def _():
        grad_ref[:, :LANES] = (dq_turned[...] * scale).T.astype(bf16)
        fetch.wait()
        weight_ref[...] = dot(x_here[...], grad_ref[...])


def attend_back(qkv, bias, grads, out, lse, turned, held, pair, within, scale, key_block, block):
    rows = qkv.shape[0]
    features = turned.shape[0]
    whole = lambda n: pl.BlockSpec((rows, LANES), lambda j: (0, n))
    part = lambda n: pl.BlockSpec((key_block, LANES), lambda j: (j, n))
    return pl.pallas_call(
        functools.partial(attend_back_kernel, scale=scale, block=block),
        grid=(rows // key_block,),
        in_specs=[
            whole(3 * pair),
            part(3 * pair + 1),
            part(3 * pair + 2),
            part(0),
            whole(pair),
            whole(within),
            pl.BlockSpec((1, 8, rows), lambda j: (within, 0, 0)),
        ]
        + [pl.BlockSpec(memory_space=pl.ANY)] * (1 + len(held)),
        out_specs=[
            pl.BlockSpec((rows, 3 * LANES), lambda j: (0, pair)),
            pl.BlockSpec((features, 3 * LANES), lambda j: (0, 0)),
        ],
        out_shape=[
            jax.ShapeDtypeStruct(qkv.shape, bf16),
            jax.ShapeDtypeStruct((features, 3 * LANES), f32),
        ],
        input_output_aliases={8: 0} if held else {},
        scratch_shapes=[pltpu.VMEM((rows, LANES), bf16)] * 6
        + [pltpu.VMEM((8, rows), f32), pltpu.VMEM((LANES, rows), f32)]
        + [pltpu.VMEM(turned.shape, bf16), pltpu.SemaphoreType.DMA(())],
        compiler_params=pltpu.CompilerParams(vmem_limit_bytes=56 << 20),
        cost_estimate=pl.CostEstimate(
            flops=40 * rows * rows * LANES,
            bytes_accessed=16 * rows * LANES,
            transcendentals=rows * rows * 2,
        ),
        name="attend_back",
    )(qkv, qkv, qkv, bias, grads, out, lse, turned, *held)


BITS = {"zh": 16, "zl": 8, "x": 4, "y": 2, "c": 1}


def number():
    return lax.axis_index("dp") * 4 + lax.axis_index("fsdp")


def bit(name):
    return jnp.minimum(lax.bitwise_and(number(), BITS[name]), 1)


def flip(value, name):
    return lax.ppermute(value, BOTH, [(n, n ^ BITS[name]) for n in range(32)])


def after(value, *others):
    return lax.optimization_barrier((value,) + others)[0]


def grow(block, name):
    return jnp.concatenate([block, flip(block, name)], axis=0)


def in_order(block, names):
    chip = lax.div(number(), 2)
    every = lax.iota(jnp.int32, block.shape[0])
    relative = lax.bitwise_xor(every, chip)
    index = lax.rem(lax.div(chip, 4) - lax.div(every, 4) + 4, 4)
    for place, name in enumerate(names):
        index = index + jnp.minimum(lax.bitwise_and(relative, BITS[name] // 2), 1) * (4 << place)
    return jnp.take(block, index, axis=0)


def pick(value, axis, index):
    return lax.squeeze(lax.dynamic_slice_in_dim(value, index, 1, axis), (axis,))


def along_z(value, amount):
    pairs = []
    for n in range(32):
        place = n // 8
        pairs.append((n, n + ((place + amount) % 4 - place) * 8))
    return lax.ppermute(value, BOTH, pairs)


def z_place():
    return lax.div(number(), 8)


class Falling:
    def __init__(self, value, axes=("z", "x", "y")):
        self.axes = list(axes)
        if value.ndim == 2:
            value = value.reshape((4, 2, 2, value.shape[0] // 16) + value.shape[1:])
        self.value = value
        self.held = [("value", 1)]

    def arrays(self, new=None):
        if new is not None:
            for name, count in self.held:
                part, new = new[:count], new[count:]
                setattr(self, name, part[0] if name in ("value", "kept") else part)
        return [
            array
            for name, _ in self.held
            for array in (
                [getattr(self, name)] if name in ("value", "kept") else getattr(self, name)
            )
        ]

    def cut(self, name):
        axis = self.axes.index(name)
        self.axes.pop(axis)
        if name == "z":
            own = z_place()
            self.pieces = [
                pick(self.value, axis, lax.rem(own + n, 4)).astype(bf16) for n in (1, 2, 3)
            ]
        else:
            own = bit(name)
            self.pieces = [pick(self.value, axis, 1 - own).astype(bf16)]
        self.kept = pick(self.value, axis, own)
        self.name = name
        self.held = [("pieces", len(self.pieces)), ("kept", 1)]

    def send(self):
        if self.name == "z":
            self.arrived = [along_z(p, n) for n, p in zip((1, 2, 3), self.pieces)]
        else:
            self.arrived = [flip(self.pieces[0], self.name)]
        self.held = [("arrived", len(self.arrived)), ("kept", 1)]

    def add(self):
        total = self.kept.astype(f32)
        for part in self.arrived:
            total = total + part.astype(f32)
        self.value = total.astype(bf16) if self.axes else total
        self.held = [("value", 1)]


def fence(values, falls=()):
    flat = list(values)
    for f in falls:
        flat += f.arrays()
    flat = list(lax.optimization_barrier(tuple(flat)))
    values, flat = flat[: len(values)], flat[len(values) :]
    for f in falls:
        count = len(f.arrays())
        f.arrays(flat[:count])
        flat = flat[count:]
    return values


def normalize(resid):
    average = jnp.mean(resid, axis=-1, keepdims=True)
    centred = resid - average
    second = jnp.mean(centred * centred, axis=-1, keepdims=True)
    inverse = lax.rsqrt(second + EPSILON)
    return centred * inverse, inverse


def normalize_back(grad, unit, inverse, gain):
    scaled = grad * gain
    along = jnp.mean(scaled * unit, axis=-1, keepdims=True)
    return inverse * (scaled - jnp.mean(scaled, axis=-1, keepdims=True) - unit * along)


def shards(
    tokens, teacher, lengths, dealing,
    query_weight, key_weight, value_weight, output_weight, inner_weight, outer_weight,
    query_bias, value_bias, output_bias, norm_gain, norm_shift, inner_bias, outer_bias,
    final_gain, final_shift,
):
    slots, row_count, width = tokens.shape
    sections = lax.axis_size("fsdp")
    dp_count = lax.axis_size("dp")
    devices = dp_count * sections
    ranks = sections // 2
    fast = dp_count == 8 and sections == 4
    hidden_units = inner_weight.shape[1]
    head_width = width // HEADS
    scale = 1.0 / math.sqrt(head_width)
    seq_total = lengths.shape[0]
    seq_len = row_count * sections
    share = width // ranks
    pairs = -(-share // LANES)
    rows = 2 * row_count
    small = query_weight.shape[0]

    place = lax.axis_index("fsdp")
    side = lax.div(place, ranks)
    rank = lax.rem(place, ranks)
    across = [(f, (f + ranks) % sections) for f in range(sections)]
    groups = [[g * ranks + r for r in range(ranks)] for g in range(2)]
    partner = [(f, f ^ 1) for f in range(sections)]
    length = lax.dynamic_index_in_dim(
        lengths, lax.axis_index("dp") * slots + side, keepdims=False
    )

    def to_swap(whole):
        kept = lax.dynamic_index_in_dim(whole, side, 0, keepdims=False)
        sent = lax.dynamic_index_in_dim(whole, 1 - side, 0, keepdims=False)
        return kept, sent

    def swap_in(whole):
        kept, sent = to_swap(whole)
        return jnp.concatenate([kept, lax.ppermute(sent, "fsdp", across)], axis=0)

    def swap_out(local):
        arrived = lax.ppermute(local[row_count:], "fsdp", across)
        kept = local[:row_count]
        whole = jnp.where(side == 0, jnp.stack([kept, arrived]), jnp.stack([arrived, kept]))
        return whole, arrived

    def other(value):
        return lax.ppermute(value, "fsdp", partner)

    def in_rank_order(mine, theirs, axis):
        return jnp.where(
            rank == 0,
            jnp.concatenate([mine, theirs], axis=axis),
            jnp.concatenate([theirs, mine], axis=axis),
        )

    def by_pairs(value):
        fill = pairs * LANES - share
        if fill:
            value = jnp.pad(value, ((0, 0),) * (value.ndim - 1) + ((0, fill),))
        return value.reshape(value.shape[:-1] + (pairs, LANES))

    if ranks == 2:
        rank_order = [rank, 1 - rank]
    else:
        rank_order = [jnp.int32(r) for r in range(ranks)]
    within = lax.iota(jnp.int32, row_count)

    def positions_of(r):
        return jnp.concatenate(
            [(side * ranks + r) * row_count + within, ((1 - side) * ranks + r) * row_count + within]
        )

    positions = jnp.concatenate([positions_of(r) for r in rank_order])
    bias = jnp.where(positions < length, 0.0, MASKED).astype(bf16)
    key_bias = jnp.broadcast_to(bias[:, None], (rows * ranks, LANES))

    vectors = [
        query_bias, value_bias, output_bias, norm_gain, norm_shift, outer_bias, final_gain,
        final_shift, inner_bias,
    ]
    lines = jnp.concatenate([v.reshape(-1, small) for v in vectors], axis=0)
    if fast:

        def columns(which):
            parts = [
                lax.dynamic_slice_in_dim(w, which * share + p * LANES, LANES, 1)
                for p in range(pairs)
                for w in (query_weight, key_weight, value_weight)
            ]
            spare = ((0, small - lines.shape[0]), (0, LANES - small))
            return jnp.concatenate(parts + [jnp.pad(lines, spare)], axis=1)

        mine, theirs = columns(rank), other(columns(1 - rank))
        first = jnp.where(rank == 0, jnp.stack([mine, theirs]), jnp.stack([theirs, mine]))[None]
        kept, sent = to_swap(tokens)
        first, sent = fence([first, sent])
        around = [along_z(first, n) for n in (1, 2, 3)]
        arrived = lax.ppermute(sent, "fsdp", across)
        *around, arrived = fence([*around, arrived])
        risen = jnp.concatenate([first] + around, axis=0)
        local = jnp.concatenate([kept, arrived], axis=0)
        cut = 5 * LANES
        left, right, local, teacher = fence([risen[..., :cut], risen[..., cut:], local, teacher])
        l_arrived, r_arrived, gathered = flip(left, "x"), flip(right, "y"), other(local)
        l_arrived, r_arrived, gathered = fence([l_arrived, r_arrived, gathered])
        gathered = jnp.concatenate([local, gathered], axis=0)
        left, right = fence(
            [jnp.concatenate([left, l_arrived], axis=0), jnp.concatenate([right, r_arrived], axis=0)]
        )
        left = grow(left, "y")
        right = grow(right, "x")
        whole = jnp.concatenate(
            [in_order(left, ["x", "y"]), in_order(right, ["y", "x"])], axis=3
        ).reshape(width, 3 * share + LANES)
        qkv_weight = whole[:, : 3 * share]
        lines = whole[:, 3 * share :].reshape(devices, small, LANES)[:, : lines.shape[0], :small]
    else:
        local = swap_in(tokens)
        gathered = lax.all_gather(
            local, "fsdp", axis=0, tiled=True, axis_index_groups=groups
        )
        whole = [
            lax.all_gather(w, BOTH, axis=0, tiled=True)
            for w in (query_weight, key_weight, value_weight)
        ]
        whole = [
            by_pairs(lax.dynamic_slice_in_dim(w, rank * share, share, 1)) for w in whole
        ]
        qkv_weight = jnp.stack(whole, axis=2).reshape(width, pairs * 3 * LANES)
        lines = lax.all_gather(lines, BOTH, axis=0, tiled=False)
    unpacked = []
    start = 0
    for vector in vectors:
        count = vector.shape[0] // small
        unpacked.append(lines[:, start : start + count].reshape(-1).astype(f32))
        start += count
    b_query, b_value, b_output, gain_one, shift_one, b_outer, gain_two, shift_two, b_inner = unpacked
    ratio = hidden_units // width
    late = jnp.concatenate(
        [output_weight]
        + [inner_weight[:, n * width : (n + 1) * width] for n in range(ratio)]
        + [outer_weight],
        axis=0,
    )
    late = lax.all_gather(late, BOTH, axis=0, tiled=False)
    w_output = late[:, :small].reshape(width, width)
    w_inner = jnp.concatenate(
        [
            late[:, (n + 1) * small : (n + 2) * small].reshape(width, width)
            for n in range(ratio)
        ],
        axis=1,
    )
    w_outer = late[:, (ratio + 1) * small :].reshape(hidden_units, width)

    slot_ids = lax.iota(jnp.int32, seq_total)
    inverse = jnp.sum(
        jnp.where(dealing[None, :] == slot_ids[:, None], slot_ids[None, :], 0), axis=1
    )
    target = lax.all_to_all(teacher, "dp", split_axis=1, concat_axis=0, tiled=True)

    b_own = [
        by_pairs(lax.dynamic_slice_in_dim(b, rank * share, share)) for b in (b_query, b_value)
    ]
    b_qkv = jnp.stack([b_own[0], jnp.zeros_like(b_own[0]), b_own[1]], axis=1).reshape(-1)
    qkv = (dot(gathered, qkv_weight) + b_qkv).astype(bf16)
    early = min(2, pairs)
    outs = [attend(qkv, key_bias, 0, early, scale, min(1024, rows * ranks))]
    if pairs > early:
        target, qkv = fence([jnp.take(after(target, outs[0][0]), inverse, axis=0), qkv])
        outs.append(attend(qkv, key_bias, early, pairs - early, scale, min(1024, rows * ranks)))
    else:
        target = jnp.take(target, inverse, axis=0)
    heads_out = jnp.concatenate([o for o, _ in outs], axis=1)[:, :share]
    if ranks == 2:
        attn_rows = in_rank_order(heads_out[:rows], other(heads_out[rows:]), 1)
    else:
        attn_rows = lax.all_to_all(
            heads_out, "fsdp", split_axis=0, concat_axis=1, tiled=True, axis_index_groups=groups
        )
    target = lax.all_to_all(target, "dp", split_axis=0, concat_axis=1, tiled=True)

    resid_one = local.astype(f32) + dot(attn_rows, w_output) + b_output
    unit_one, inverse_one = normalize(resid_one)
    hidden = (unit_one * gain_one + shift_one).astype(bf16)
    target = swap_in(after(target, hidden))
    inner = dot(hidden, w_inner) + b_inner
    normal = 0.5 + 0.5 * lax.erf(inner * math.sqrt(0.5))
    act = (inner * normal).astype(bf16)
    slope = (
        normal + inner * jnp.exp(-0.5 * inner * inner) * (1.0 / math.sqrt(2 * math.pi))
    ).astype(bf16)
    resid_two = hidden.astype(f32) + dot(act, w_outer) + b_outer
    unit_two, inverse_two = normalize(resid_two)
    final = unit_two * gain_two + shift_two
    output, output_arrived = swap_out(final.astype(bf16))

    valid = (positions_of(rank) < length).astype(f32)[:, None]
    loss_scale = seq_total * seq_len / jnp.sum(lengths).astype(f32)
    grad_final = loss_scale * (final - target.astype(f32)) * valid
    grad_gain_two = jnp.sum(grad_final * unit_two, axis=0)
    grad_shift_two = jnp.sum(grad_final, axis=0)
    d_two = normalize_back(grad_final, unit_two, inverse_two, gain_two)
    d_out = d_two.astype(bf16)
    grad_outer_bias = jnp.sum(d_out.astype(f32), axis=0)
    outer_sum = dot(act, d_out, TN).astype(bf16)
    grad_outer = lax.psum_scatter(outer_sum, BOTH, scatter_dimension=0, tiled=True).astype(f32)
    d_inner = (dot(d_out, w_outer, NT) * slope.astype(f32)).astype(bf16)
    grad_inner_bias = jnp.sum(d_inner.astype(f32), axis=0)
    d_hidden = d_two + dot(d_inner, w_inner, NT)
    grad_gain_one = jnp.sum(d_hidden * unit_one, axis=0)
    grad_shift_one = jnp.sum(d_hidden, axis=0)
    d_one = normalize_back(d_hidden, unit_one, inverse_one, gain_one)
    d_mix = d_one.astype(bf16)
    grad_output_bias = jnp.sum(d_mix.astype(f32), axis=0)
    d_attn = dot(d_mix, w_output, NT).astype(bf16)
    if ranks == 2:
        cut = lambda r: lax.dynamic_slice_in_dim(d_attn, r * share, share, 1)
        heads_grad = jnp.concatenate([cut(rank), other(cut(1 - rank))], axis=0)
    else:
        heads_grad = lax.all_to_all(
            d_attn, "fsdp", split_axis=1, concat_axis=0, tiled=True, axis_index_groups=groups
        )
    heads_grad = by_pairs(heads_grad).reshape(rows * ranks, pairs * LANES)

    if fast:
        def halves(left, right):
            wide = right.shape[1] // 2
            cut = lambda r: lax.dynamic_slice_in_dim(right, r * wide, wide, 1)
            sent = other(dot(left, cut(1 - rank), TN).astype(bf16))
            return (dot(left, cut(rank), TN) + sent.astype(f32)).astype(bf16)

        inner_half = halves(hidden, d_inner)
        output_half = halves(attn_rows, d_mix)
        cut_at = hidden_units // 4 + 2 * LANES
        falls = [
            Falling(inner_half[:, :cut_at]),
            Falling(jnp.concatenate([inner_half[:, cut_at:], output_half], axis=1)),
        ]
        moves = [(falls[0], "x"), (falls[1], "y")]
        keep = [outer_sum, output_arrived]
    else:
        grad_inner = lax.psum_scatter(
            dot(hidden, d_inner, TN), BOTH, scatter_dimension=0, tiled=True
        )
        grad_output = lax.psum_scatter(
            dot(attn_rows, d_mix, TN), BOTH, scatter_dimension=0, tiled=True
        )

    turned = jnp.concatenate([gathered.T, jnp.ones((16, rows * ranks), bf16)], axis=0)
    held = []
    weight_falls, parts = [], []
    for pair in range(pairs):
        out, lse = outs[pair // early]
        if fast:
            for f, name in moves:
                f.cut(name)
            everything = falls + weight_falls
            heads_grad, *_ = fence([heads_grad] + (keep if pair == 0 else []), everything)
            for f, _ in moves:
                f.send()
        d_qkv, weights = attend_back(
            qkv, key_bias, heads_grad, out, lse, turned, held, pair, pair % early, scale, 512, 1024
        )
        if fast:
            d_qkv, weights, heads_grad = fence([d_qkv, weights, heads_grad], everything)
            for f, _ in moves:
                f.add()
            if pair < 2:
                weight_falls.append(Falling(weights[:width].astype(bf16)))
            if pair == 0:
                moves = [(falls[0], "y"), (falls[1], "x"), (weight_falls[0], "x")]
            if pair == 1:
                both = jnp.concatenate([falls[0].value, falls[1].value], axis=2)
                falls = [Falling(both, ["z"])]
                moves = [(falls[0], "z"), (weight_falls[0], "y"), (weight_falls[1], "x")]
        held = [d_qkv]
        parts.append(weights)

    def place_share(part):
        empty = jnp.zeros((width,), f32)
        return lax.dynamic_update_slice_in_dim(empty, part, rank * share, 0)

    biases = jnp.stack([p[width].reshape(3, LANES) for p in parts], axis=1)
    biases = biases.reshape(3, pairs * LANES)[:, :share]
    sums = [
        place_share(biases[0]), place_share(biases[2]), grad_output_bias, grad_gain_one,
        grad_shift_one, grad_outer_bias, grad_gain_two, grad_shift_two, grad_inner_bias,
    ]
    sums = jnp.concatenate([s.reshape(devices, -1) for s in sums], axis=1)

    if fast:
        count = sums.shape[1]
        deep = 2 * count
        wide = 3 * LANES
        sums = jnp.pad(sums.reshape(16, deep), ((0, 0), (0, 8 * wide - deep)))
        last = jnp.concatenate(
            [parts[-1][:width].reshape(16, 2 * small, wide), sums.reshape(16, 8, wide)], axis=1
        )
        weight_falls.append(Falling(last.astype(bf16).reshape(-1, wide)))
        moves = [(weight_falls[1], "y"), (weight_falls[2], "x")]
        for f, name in moves:
            f.cut(name)
        (d_qkv,) = fence([d_qkv], weight_falls)
        for f, _ in moves:
            f.send()
        d_gathered = dot(d_qkv, qkv_weight, NT)
        (d_gathered,) = fence([d_gathered], weight_falls)
        for f, _ in moves:
            f.add()
        weight_falls[2].cut("y")
        (d_sent,) = fence([d_gathered[rows:].astype(bf16)], weight_falls)
        weight_falls[2].send()
        d_arrived = other(d_sent)
        (d_arrived,) = fence([d_arrived], weight_falls)
        weight_falls[2].add()
        grad_rows = (d_one + d_gathered[:rows] + d_arrived.astype(f32)).astype(bf16)
        three = Falling(
            jnp.concatenate(
                [jnp.concatenate([f.value[:, : 2 * small] for f in weight_falls], axis=2)]
                + [
                    jnp.pad(
                        weight_falls[2].value[:, 2 * small :],
                        ((0, 0), (0, 0), (0, (pairs - 1) * wide)),
                    )
                ],
                axis=1,
            ),
            ["z"],
        )
        three.cut("z")
        (grad_rows,) = fence([grad_rows], [three])
        three.send()
        input_grad, _ = swap_out(grad_rows)
        three.add()

        def settle(value):
            value = value.reshape(2, small, value.shape[1])
            return pick(value, 0, rank), other(pick(value, 0, 1 - rank))

        mine, theirs = settle(falls[0].value)
        whole = in_rank_order(mine[:, : hidden_units // 2], theirs[:, : hidden_units // 2], 1)
        grad_inner = whole
        grad_output = in_rank_order(mine[:, hidden_units // 2 :], theirs[:, hidden_units // 2 :], 1)
        own, theirs = settle(three.value[: 2 * small])
        own = own.reshape(small, pairs, 3, LANES)
        theirs = theirs.reshape(small, pairs, 3, LANES)
        value = in_rank_order(own, theirs, 1)
        grad_query, grad_key, grad_value = [
            value[:, :, n].reshape(small, width) for n in range(3)
        ]
        tail = three.value[2 * small :, :wide]
        sums = (tail + other(tail)).reshape(-1)[:deep].reshape(2, count)
        sums = pick(sums, 0, rank)
    else:
        d_gathered = dot(d_qkv, qkv_weight, NT)
        if ranks == 2:
            d_local = d_gathered[:rows] + other(d_gathered[rows:].astype(bf16)).astype(f32)
        else:
            d_local = lax.psum_scatter(
                d_gathered, "fsdp", scatter_dimension=0, tiled=True, axis_index_groups=groups
            )
        input_grad, _ = swap_out((d_one + d_local).astype(bf16))
        value = jnp.stack([p[:width].reshape(width, 3, LANES) for p in parts], axis=2)
        value = value.reshape(width, 3, pairs * LANES)[:, :, :share]
        empty = jnp.zeros((width, 3, width), f32)
        value = lax.dynamic_update_slice_in_dim(empty, value, rank * share, 2)
        grad_query, grad_key, grad_value = [
            lax.psum_scatter(value[:, n], BOTH, scatter_dimension=0, tiled=True)
            for n in range(3)
        ]
        sums = lax.psum_scatter(sums, BOTH, scatter_dimension=0, tiled=True).reshape(-1)
    split = []
    start = 0
    for vector in vectors:
        count = vector.shape[0]
        split.append(sums[start : start + count])
        start += count
    return (
        output, input_grad, grad_query, grad_key, grad_value, grad_output, grad_inner, grad_outer,
        split[0], split[1], split[2], split[3], split[4], split[8], split[5], split[6], split[7],
    )


def solution(mesh):
    act = P("dp", "fsdp", None)
    matrix = P(BOTH, None)
    vector = P(BOTH)
    return jax.shard_map(
        shards,
        mesh=mesh,
        in_specs=(act, act, P(), P()) + (matrix,) * 6 + (vector,) * 9,
        out_specs=(act, act) + (matrix,) * 6 + (vector,) * 9,
        check_vma=False,
    )
```
